32 devices in a mesh: tm: 8 (over y, x, core), elem: 4 (over z).
Axes of the slice: x: 2, y: 2, z: 4, core: 2. Of those that a mesh axis runs over, the one named last changes fastest.
Arguments:
- samples: float32 [2, 512, 24576], P(None, 'elem', 'tm'), may hold values from -24 to 24
- shift_bin: int32 [1], replicated, may hold values from 1 to 63
- start_vectors: int32 [2, 512, 64], P(None, 'elem'), may hold values from 0 to 8
- tap_table: int32 [4, 1024], replicated, may hold values from -2048 to 2047
Outputs:
- spectra: float32 [2, 64, 24, 1024], P(None, 'elem', 'tm')
- weights: float32 [2, 512, 64], P(None, 'elem')
The draws below stay inside these ranges and needn't reach their ends.
All inputs are finite; a program needn't handle non-finite values.
Results may differ from the reference program's by a relative error of at most 0.0003.
Values sent between devices are 32-bit elements; how exact they have to be, the bound alone decides.
No kernel may reach another device: no remote copies, remote signals or barrier semaphores. Data moves between devices by JAX's collectives and lax.ppermute only.
A program may use at most 128 MiB of HBM per device.

```python
import math
import jax
import jax.numpy as jnp
from jax import lax

ELEMS = 512
BEAMS = 64
CHANNELS = 1024
TAPS = 4
ITERS = 3
SPAN = 3072
SAMPLES = 24576


def draw_samples(key, part):
    keys = jax.random.split(jax.random.fold_in(key, 71), 2)
    noise = jnp.clip(jax.random.normal(keys[0], (2, ELEMS, SAMPLES), jnp.float32), -5.0, 5.0)
    scales = jnp.exp(jax.random.uniform(keys[1], (ELEMS,), jnp.float32, math.log(0.5), math.log(2.0)))
    ramp = 0.6 + 1.2 * jnp.arange(SAMPLES, dtype=jnp.float32) / SAMPLES
    return jnp.clip(noise * scales[None, :, None] * ramp[None, None, :], -24.0, 24.0)


def plant(result, key, least, high):
    longest = result.shape.index(max(result.shape))
    spots = []
    for shift in (0, 1):
        where = [jax.random.randint(jax.random.fold_in(key, axis), (), 0, length) for axis, length in enumerate(result.shape)]
        where[longest] = (where[longest] + shift) % result.shape[longest]
        spots.append(tuple(where))
    return result.at[spots[0]].set(least).at[spots[1]].set(high)


def setup_inputs(seed: int = 0) -> dict:
    key_of = jax.random.split(jax.random.key(seed), 5)
    samples = draw_samples(jax.random.fold_in(key_of[4], 71), 0)
    shift_bin = jax.random.randint(key_of[1], (1,), 1, 64).astype(jnp.int32)
    start_vectors = plant(jax.random.randint(key_of[2], (2, ELEMS, BEAMS), 0, 9), jax.random.fold_in(key_of[2], 1), 0, 8).astype(jnp.int32)
    tap_table = plant(jax.random.randint(key_of[3], (TAPS, CHANNELS), -2048, 2048), jax.random.fold_in(key_of[3], 1), -2048, 2047).astype(jnp.int32)
    return {"samples": samples, "shift_bin": shift_bin, "start_vectors": start_vectors, "tap_table": tap_table}


EPS = 1e-06
HIGH = lax.Precision.HIGHEST

def rotation(shift_bin, offset, count, modulus):
    times = offset + lax.iota(jnp.int32, count)
    folded = shift_bin[0] * times % modulus
    angle = 2.0 * math.pi / modulus * folded.astype(jnp.float32)
    return (jnp.cos(angle), jnp.sin(angle))

def stacked_left(sig_real, sig_imag, cos_table, sin_table):
    mod_real = sig_real * cos_table + sig_imag * sin_table
    mod_imag = sig_imag * cos_table - sig_real * sin_table
    return jnp.concatenate([sig_real, sig_imag, mod_real, mod_imag], 0)

def split_grams(grams, row_count, col_count):

    def block(row_block, col_block):
        return grams[row_block * row_count:(row_block + 1) * row_count, col_block * col_count:(col_block + 1) * col_count]
    return jnp.stack([block(0, 0) + block(1, 1), block(1, 0) - block(0, 1), block(2, 0) + block(3, 1), block(3, 0) - block(2, 1)])

def contract(left_rows, right_rows):
    return lax.dot_general(left_rows, right_rows, (((1,), (1,)), ((), ())), precision=HIGH, preferred_element_type=jnp.float32)

def matmul(left_rows, right_rows):
    return jnp.dot(left_rows, right_rows, precision=HIGH, preferred_element_type=jnp.float32)

def normalize(vector):
    squares = lax.optimization_barrier(jnp.sum(vector * vector, axis=(0, 1)))
    return vector / jnp.sqrt(squares + EPS)

def reference(samples, shift_bin, start_vectors, tap_table):
    total = samples.shape[2]
    elems = samples.shape[1]
    block_len = SPAN
    block_count = total // block_len

    def accumulate(index, grams):
        begin = (index * block_len).astype(jnp.int32)
        piece = lax.dynamic_slice_in_dim(samples, begin, block_len, 2)
        cos_table, sin_table = rotation(shift_bin, begin, block_len, total)
        left_rows = stacked_left(piece[0], piece[1], cos_table, sin_table)
        right_rows = jnp.concatenate([piece[0], piece[1]], 0)
        return grams + contract(left_rows, right_rows)
    grams = lax.fori_loop(0, block_count, accumulate, jnp.zeros((4 * elems, 2 * elems), jnp.float32))
    corr = split_grams(grams, elems, elems)
    plain_real = corr[0] / total
    plain_imag = corr[1] / total
    cyc_scale = 1.0 / math.sqrt(total * elems)
    cyc_real = corr[2] * cyc_scale
    cyc_imag = corr[3] * cyc_scale
    vector = normalize(start_vectors.astype(jnp.float32) - 4.5)
    for iteration in range(ITERS):
        vec_real, vec_imag = (vector[0], vector[1])
        adj_real = matmul(cyc_real.T, vec_real) + matmul(cyc_imag.T, vec_imag)
        adj_imag = matmul(cyc_real.T, vec_imag) - matmul(cyc_imag.T, vec_real)
        out_real = matmul(cyc_real, adj_real) - matmul(cyc_imag, adj_imag) + matmul(plain_real, vec_real) - matmul(plain_imag, vec_imag)
        out_imag = matmul(cyc_real, adj_imag) + matmul(cyc_imag, adj_real) + matmul(plain_real, vec_imag) + matmul(plain_imag, vec_real)
        vector = normalize(jnp.stack([out_real, out_imag]))
    vec_real, vec_imag = (vector[0], vector[1])
    beam_real = matmul(vec_real.T, samples[0]) + matmul(vec_imag.T, samples[1])
    beam_imag = matmul(vec_real.T, samples[1]) - matmul(vec_imag.T, samples[0])
    beam_series = jnp.stack([beam_real, beam_imag])
    rim = (TAPS - 1) * CHANNELS
    padded = jnp.pad(beam_series, ((0, 0), (0, 0), (rim, 0)))
    frames = total // CHANNELS
    shaped = padded.reshape(2, beam_series.shape[1], TAPS - 1 + frames, CHANNELS)
    taps = tap_table.astype(jnp.float32) / 2048.0
    folded = jnp.zeros((2, beam_series.shape[1], frames, CHANNELS), jnp.float32)
    for tap in range(TAPS):
        folded = folded + taps[tap] * shaped[:, :, TAPS - 1 - tap:TAPS - 1 - tap + frames, :]
    spectrum = jnp.fft.fft(folded[0] + 1j * folded[1], axis=-1) / math.sqrt(CHANNELS)
    spectra = jnp.stack([jnp.real(spectrum), jnp.imag(spectrum)]).astype(folded.dtype)
    return (spectra, vector)
```

```python
import math

import jax
import jax.numpy as jnp
from jax import lax
from jax.experimental import pallas as pl
from jax.experimental.pallas import tpu as pltpu
from jax.sharding import PartitionSpec as P

ITERS = 3
EPS = 1e-06
F32 = jnp.float32
BF16 = jnp.bfloat16
NT = (((1,), (1,)), ((), ()))
NN = (((1,), (0,)), ((), ()))


def shifted(x, axis, by):
    devices = lax.axis_size(axis)
    return lax.ppermute(x, axis, [(i, (i + by) % devices) for i in range(devices)])


def swapped(x, axis, bit):
    devices = lax.axis_size(axis)
    return lax.ppermute(x, axis, [(i, i ^ (1 << bit)) for i in range(devices)])


def from_behind(x, axis, by):
    devices = lax.axis_size(axis)
    pairs = [(i, i + by) for i in range(devices) if 0 <= i + by < devices]
    return lax.ppermute(x, axis, pairs)


def halves(x, flag):
    count = x.shape[0] // 2
    keep = lax.dynamic_slice_in_dim(x, flag * count, count, 0)
    send = lax.dynamic_slice_in_dim(x, (1 - flag) * count, count, 0)
    return keep, send


def bit_of(index, bit):
    return (index >> bit) & 1


def joined(own, other, flag):
    return jnp.where(
        flag == 0, jnp.concatenate([own, other], 0), jnp.concatenate([other, own], 0)
    )


def scatter_step(x, axis, bit):
    keep, send = halves(x, bit_of(lax.axis_index(axis), bit))
    return keep + swapped(send, axis, bit)


def gather_step(x, axis, bit):
    return joined(x, swapped(x, axis, bit), bit_of(lax.axis_index(axis), bit))


def summed_everywhere(x):
    tm_bits = list(range(int(math.log2(lax.axis_size("tm")))))
    elem_bits = list(range(int(math.log2(lax.axis_size("elem")))))
    first, rest = tm_bits[:1], tm_bits[1:]
    orders = (rest, rest[::-1])
    for bit in first:
        x = scatter_step(x, "tm", bit)
    half = x.shape[0] // 2
    parts = [x[:half], x[half:]]
    for step in range(len(rest)):
        parts = [scatter_step(part, "tm", order[step]) for part, order in zip(parts, orders)]
    flag = bit_of(lax.axis_index("elem"), 0)
    keep = jnp.where(flag == 0, parts[0], parts[1])
    send = jnp.where(flag == 0, parts[1], parts[0])
    x = keep + swapped(send, "elem", 0)
    for bit in elem_bits[1:]:
        x = scatter_step(x, "elem", bit)
    for bit in elem_bits[:0:-1]:
        x = gather_step(x, "elem", bit)
    other = swapped(x, "elem", 0)
    parts = [jnp.where(flag == 0, x, other), jnp.where(flag == 0, other, x)]
    for step in range(len(rest) - 1, -1, -1):
        parts = [gather_step(part, "tm", order[step]) for part, order in zip(parts, orders)]
    x = jnp.concatenate(parts, 0)
    for bit in first:
        x = gather_step(x, "tm", bit)
    return x


def split(x):
    high = x.astype(BF16)
    return high, (x - high.astype(F32)).astype(BF16)


def split_kept(x):
    high = lax.reduce_precision(x, 8, 7)
    return high.astype(BF16), (x - high).astype(BF16)


def dot(left, right, dims):
    return lax.dot_general(left, right, dims, preferred_element_type=F32)


def triple(left, right, dims):
    return (
        dot(left[0], right[0], dims) + dot(left[0], right[1], dims) + dot(left[1], right[0], dims)
    )


def gram_kernel(has_acc, place_ref, *refs):
    pieces = refs[:4]
    cs_ref = refs[4]
    if has_acc:
        acc_ref = refs[5]
        refs = refs[6:]
    else:
        acc_ref = None
        refs = refs[5:]
    out_ref, lefts = refs[0], refs[1:]
    n = pieces[0].shape[1]
    count = pieces[0].shape[2]
    elems = n * len(pieces)
    for k, piece in enumerate(pieces):
        rows = pl.ds(pl.multiple_of(place_ref[k] * n, n), n)
        real, imag = piece[0], piece[1]
        cosine, sine = cs_ref[0:1, :], cs_ref[1:2, :]
        mod_real = real * cosine + imag * sine
        mod_imag = imag * cosine - real * sine
        real, imag, mod_real, mod_imag = split(real), split(imag), split(mod_real), split(mod_imag)
        for part in range(2):
            for where, (a, b) in enumerate(
                (
                    (real[part], imag[part]),
                    (mod_real[part], mod_imag[part]),
                    (mod_imag[part], -mod_real[part]),
                    (imag[part], -real[part]),
                )
            ):
                ref = lefts[2 * where + part]
                ref[rows, 0:count] = a
                ref[rows, count:] = b

    def product(where, top, height, left, width):
        a = tuple(lefts[2 * where + part][pl.ds(top, height), :] for part in range(2))
        b = tuple(lefts[part][pl.ds(left, width), :] for part in range(2))
        return triple(a, b, NT)

    def put(top, height, left, width, value):
        if acc_ref is not None:
            value = value + acc_ref[pl.ds(top, height), pl.ds(left, width)]
        out_ref[pl.ds(top, height), pl.ds(left, width)] = value

    half = elems // 2
    for top in (0, half):
        put(top, half, 0, elems, product(1, top, half, 0, elems))
        put(elems + top, half, 0, elems, product(2, top, half, 0, elems))
    base = 2 * elems
    put(base, half, half, half, product(0, 0, half, half, half))
    put(base + half, half, 0, half, product(3, half, half, 0, half))
    above = lax.broadcasted_iota(jnp.int32, (half, half), 0) <= lax.broadcasted_iota(
        jnp.int32, (half, half), 1
    )
    for top in (0, half):
        both = jnp.where(
            above, product(0, top, half, top, half), product(3, top, half, top, half)
        )
        put(base + top, half, top, half, both)


def gram(place, pieces, cs, acc):
    elems = pieces[0].shape[1] * len(pieces)
    count = pieces[0].shape[2]
    vmem = pl.BlockSpec(memory_space=pltpu.VMEM)
    args = [place, *pieces, cs] + ([] if acc is None else [acc])
    return pl.pallas_call(
        lambda *refs: gram_kernel(acc is not None, *refs),
        out_shape=jax.ShapeDtypeStruct((3 * elems, elems), F32),
        in_specs=[pl.BlockSpec(memory_space=pltpu.SMEM)] + [vmem] * (len(args) - 1),
        out_specs=vmem,
        scratch_shapes=[pltpu.VMEM((elems, 2 * count), BF16)] * 8,
        input_output_aliases={} if acc is None else {len(args) - 1: 0},
        cost_estimate=pl.CostEstimate(
            flops=2 * 21 * elems * elems * count, bytes_accessed=16 * elems * elems, transcendentals=0
        ),
        name="gram",
    )(*args)


def power_kernel(total, place_ref, corr_ref, *refs):
    starts = refs[:4]
    out_ref = refs[4]
    cr, ci, pr, pi, v_ref = refs[5:7], refs[7:9], refs[9:11], refs[11:13], refs[13]
    elems = corr_ref.shape[1]
    n = starts[0].shape[1]
    rows = starts[0].shape[0]
    beams = rows // 2
    scale = 1.0 / math.sqrt(total * elems)

    def store(pair, value):
        pair[0][...], pair[1][...] = split(value)

    store(cr, corr_ref[0:elems, :] * scale)
    store(ci, corr_ref[elems : 2 * elems, :] * scale)
    packed = corr_ref[2 * elems :, :] * (1.0 / total)
    mirrored = packed.T
    row = lax.broadcasted_iota(jnp.int32, (elems, elems), 0)
    col = lax.broadcasted_iota(jnp.int32, (elems, elems), 1)
    store(pr, jnp.where(row <= col, packed, mirrored))
    store(pi, jnp.where(row > col, packed, jnp.where(row < col, -mirrored, 0.0)))
    for k, start in enumerate(starts):
        v_ref[:, pl.ds(pl.multiple_of(place_ref[k] * n, n), n)] = start[...] - 4.5

    def normalized(v):
        squares = jnp.sum(v * v, axis=1, keepdims=True)
        squares = squares[:beams] + squares[beams:]
        inverse = 1.0 / jnp.sqrt(squares + EPS)
        return v * jnp.concatenate([inverse, inverse], 0)

    def times(v, pair, dims):
        high, low = split(v)
        both = dot(jnp.concatenate([high, low], 0), pair[0][...], dims)
        return both[:rows] + both[rows:] + dot(high, pair[1][...], dims)

    v = normalized(v_ref[...])
    for _ in range(ITERS):
        by_real = times(v, cr, NN)
        by_imag = times(v, ci, NN)
        w = jnp.concatenate(
            [by_real[:beams] + by_imag[beams:], by_real[beams:] - by_imag[:beams]], 0
        )
        by_real = times(w, cr, NT) + times(v, pr, NT)
        by_imag = times(w, ci, NT) + times(v, pi, NT)
        v = normalized(
            jnp.concatenate(
                [by_real[:beams] - by_imag[beams:], by_real[beams:] + by_imag[:beams]], 0
            )
        )
    out_ref[...] = v


def power(total, place, corr, starts):
    elems = corr.shape[1]
    rows = starts[0].shape[0]
    vmem = pl.BlockSpec(memory_space=pltpu.VMEM)
    return pl.pallas_call(
        lambda *refs: power_kernel(total, *refs),
        out_shape=jax.ShapeDtypeStruct((rows, elems), F32),
        in_specs=[pl.BlockSpec(memory_space=pltpu.SMEM)] + [vmem] * (1 + len(starts)),
        out_specs=vmem,
        scratch_shapes=[pltpu.VMEM((elems, elems), BF16)] * 8 + [pltpu.VMEM((rows, elems), F32)],
        cost_estimate=pl.CostEstimate(
            flops=ITERS * 36 * elems * elems * rows, bytes_accessed=16 * elems * elems, transcendentals=0
        ),
        name="power",
    )(place, corr, *starts)


def beam_kernel(place_ref, v_ref, *refs):
    pieces, out_ref = refs[:-1], refs[-1]
    rows = v_ref.shape[0]
    beams = rows // 2
    n = pieces[0].shape[1]
    count = pieces[0].shape[2]
    lefts = []
    for k in range(4):
        v = v_ref[:, pl.ds(pl.multiple_of(place_ref[k] * n, n), n)]
        high, low = split(v)
        lefts.append((jnp.concatenate([high, low], 0), high))
    for chunk in range(len(pieces) // 4):
        totals = []
        for half in range(2):
            total = 0.0
            for k in range(4):
                high, low = split(pieces[4 * chunk + k][half])
                both = dot(lefts[k][0], high, NN)
                total = total + (both[:rows] + both[rows:] + dot(lefts[k][1], low, NN))
            totals.append(total)
        by_real, by_imag = totals
        cols = pl.ds(chunk * count, count)
        out_ref[0, :, cols] = by_real[:beams] + by_imag[beams:]
        out_ref[1, :, cols] = by_imag[:beams] - by_real[beams:]


def beams_of(place, v, pieces):
    beams = v.shape[0] // 2
    count = pieces[0].shape[2] * (len(pieces) // 4)
    vmem = pl.BlockSpec(memory_space=pltpu.VMEM)
    return pl.pallas_call(
        beam_kernel,
        out_shape=jax.ShapeDtypeStruct((2, beams, count), F32),
        in_specs=[pl.BlockSpec(memory_space=pltpu.SMEM)] + [vmem] * (1 + len(pieces)),
        out_specs=vmem,
        name="beams",
    )(place, v, *pieces)


def dft_kernel(place_ref, *refs):
    pieces = refs[:4]
    ch, cl, sh, sl, out_ref = refs[4:]
    rows = pieces[0].shape[1]
    count = pieces[0].shape[2]
    by_cos, by_sin = 0.0, 0.0
    for k, piece in enumerate(pieces):
        where = pl.ds(pl.multiple_of(place_ref[k] * count, count), count)
        high, low = split(jnp.concatenate([piece[0], piece[1]], 0))
        both = jnp.concatenate([high, low], 0)
        for table in range(2):
            t_high, t_low = ((ch, cl), (sh, sl))[table]
            value = dot(both, t_high[where, :], NN)
            value = value[: 2 * rows] + value[2 * rows :] + dot(high, t_low[where, :], NN)
            if table == 0:
                by_cos = by_cos + value
            else:
                by_sin = by_sin + value
    out_ref[0] = by_cos[:rows] + by_sin[rows:]
    out_ref[1] = by_cos[rows:] - by_sin[:rows]


def dft(place, pieces, tables):
    rows = pieces[0].shape[1]
    channels = tables[0].shape[0]
    width = 256
    whole = pl.BlockSpec(pieces[0].shape, lambda i: (0, 0, 0))
    return pl.pallas_call(
        dft_kernel,
        grid=(channels // width,),
        out_shape=jax.ShapeDtypeStruct((2, rows, channels), F32),
        in_specs=[pl.BlockSpec(memory_space=pltpu.SMEM)]
        + [whole] * 4
        + [pl.BlockSpec((channels, width), lambda i: (0, i))] * 4,
        out_specs=pl.BlockSpec((2, rows, width), lambda i: (0, 0, i)),
        name="dft",
    )(place, *pieces, *tables)


def rotation(shift_bin, times, modulus):
    folded = shift_bin[0] * times % modulus
    angle = 2.0 * math.pi / modulus * folded.astype(F32)
    return jnp.stack([jnp.cos(angle), jnp.sin(angle)])


def dft_tables(channels):
    step = 32
    f = lax.iota(jnp.int32, channels)[None, :]

    def rows(count, factor):
        k = factor * lax.iota(jnp.int32, count)[:, None] * f % channels
        angle = 2.0 * math.pi / channels * k.astype(F32)
        return jnp.cos(angle), jnp.sin(angle)

    coarse, fine = rows(channels // step, step), rows(step, 1)
    a_cos, a_sin = (t[:, None, :] for t in coarse)
    b_cos, b_sin = (t[None, :, :] for t in fine)
    norm = 1.0 / math.sqrt(channels)
    cosine = ((a_cos * b_cos - a_sin * b_sin) * norm).reshape(channels, channels)
    sine = ((a_sin * b_cos + a_cos * b_sin) * norm).reshape(channels, channels)
    return (*split_kept(cosine), *split_kept(sine))


def body(samples, shift_bin, start_vectors, tap_table):
    taps_count, channels = tap_table.shape
    span_len = samples.shape[2]
    devices = lax.axis_size("elem")
    modulus = span_len * lax.axis_size("tm")
    frames = span_len // channels
    quarter = channels // devices
    mine = lax.axis_index("elem")
    span_start = lax.axis_index("tm") * span_len
    place = jnp.stack([(mine - k) % devices for k in range(devices)])

    own_start = start_vectors.astype(F32).transpose(0, 2, 1).reshape(-1, start_vectors.shape[1])
    starts = [own_start] + [shifted(own_start, "elem", k) for k in range(1, devices)]

    chunks = []
    corr = None
    for frame in range(frames):
        own = []
        for k in range(devices):
            begin = frame * channels + (mine + k) % devices * quarter
            own.append(lax.dynamic_slice_in_dim(samples, begin, quarter, 2))
        if frame >= 2:
            own[1:], _ = lax.optimization_barrier((own[1:], chunks[frame - 2]))
        pieces = [own[0]] + [shifted(own[k], "elem", k) for k in range(1, devices)]
        times = span_start + frame * channels + mine * quarter + lax.iota(jnp.int32, quarter)
        rotated = rotation(shift_bin, times, modulus)
        if frame == 0:
            tables = dft_tables(channels)
            rotated, tables = lax.optimization_barrier((rotated, tables))
        corr = gram(place, pieces, rotated, corr)
        chunks.append(pieces)

    corr = summed_everywhere(corr)
    v = power(modulus, place, corr, starts)
    beams = v.shape[0] // 2
    elems_dev = samples.shape[1]
    weights = (
        lax.dynamic_slice_in_dim(v, mine * elems_dev, elems_dev, 1)
        .reshape(2, beams, elems_dev)
        .transpose(0, 2, 1)
    )
    b = beams_of(place, v, [piece for pieces in chunks for piece in pieces])
    extended = jnp.concatenate([from_behind(b[:, :, -(taps_count - 1) * quarter :], "tm", 1), b], 2)
    taps = lax.dynamic_slice_in_dim(tap_table, mine * quarter, quarter, 1).astype(F32) / 2048.0
    folded = []
    for frame in range(frames):
        w = 0.0
        for tap in range(taps_count):
            at = taps_count - 1 + frame - tap
            w = w + taps[tap] * extended[:, :, at * quarter : (at + 1) * quarter]
        folded.append(w)
    folded = jnp.stack(folded, 1)
    beams_dev = beams // devices
    received = []
    for k in range(devices):
        part = lax.dynamic_slice_in_dim(folded, (mine + k) % devices * beams_dev, beams_dev, 2)
        part = part.reshape(2, frames * beams_dev, quarter)
        received.append(part if k == 0 else shifted(part, "elem", k))
    spectra = dft(place, received, tables)
    spectra = spectra.reshape(2, frames, beams_dev, channels).transpose(0, 2, 1, 3)
    return (spectra, weights.reshape(2, elems_dev, beams))


def solution(mesh):
    return jax.shard_map(
        body,
        mesh=mesh,
        in_specs=(P(None, "elem", "tm"), P(), P(None, "elem", None), P()),
        out_specs=(P(None, "elem", "tm", None), P(None, "elem", None)),
        check_vma=False,
    )
```

```python
import math

import jax
import jax.numpy as jnp
from jax import lax
from jax.experimental import pallas as pl
from jax.experimental.pallas import tpu as pltpu
from jax.sharding import PartitionSpec as P


ITERS = 3
EPS = 1e-06
F32 = jnp.float32
BF16 = jnp.bfloat16
NT = (((1,), (1,)), ((), ()))
NN = (((1,), (0,)), ((), ()))


def crossed(x, axis, mask):
    return lax.ppermute(x, axis, [(i, i ^ mask) for i in range(lax.axis_size(axis))])


def swapped(x, axis, bit):
    return crossed(x, axis, 1 << bit)


def bits(axis):
    return list(range(lax.axis_size(axis).bit_length() - 1))


def from_behind(x, axis, by):
    devices = lax.axis_size(axis)
    pairs = [(i, i + by) for i in range(devices) if 0 <= i + by < devices]
    return lax.ppermute(x, axis, pairs)


def bit_of(index, bit):
    return (index >> bit) & 1


def joined(own, other, flag):
    return jnp.where(
        flag == 0, jnp.concatenate([own, other], 0), jnp.concatenate([other, own], 0)
    )


def gather_step(x, axis, bit):
    return joined(x, swapped(x, axis, bit), bit_of(lax.axis_index(axis), bit))


def summed_everywhere(keep, send):
    rest = bits("tm")[1:]
    orders = (rest, rest[::-1])
    index = lax.axis_index("tm")
    sums, cut = (keep, swapped(send, "tm", 0)), 2
    for step in range(len(rest)):
        flags = jnp.stack([bit_of(index, order[step]) for order in orders])
        kept, sent = add_split(cut, flags, *sums)
        got = [swapped(part, "tm", order[step]) for part, order in zip(sent, orders)]
        sums, cut = (kept[0], got[0], kept[1], got[1]), 1
    flag = bit_of(lax.axis_index("elem"), 0)
    x, sent = add_choose(flag, *sums)
    x = x + swapped(sent, "elem", 0)
    for bit in bits("elem")[1:]:
        x = x + swapped(x, "elem", bit)
    other = swapped(x, "elem", 0)
    parts = [jnp.where(flag == 0, x, other), jnp.where(flag == 0, other, x)]
    for step in range(len(rest) - 1, -1, -1):
        parts = [gather_step(part, "tm", order[step]) for part, order in zip(parts, orders)]
    return parts, [swapped(part, "tm", 0) for part in parts]


def split(x):
    high = x.astype(BF16)
    return high, (x - high.astype(F32)).astype(BF16)


def split_kept(x):
    high = lax.reduce_precision(x, 8, 7)
    return high.astype(BF16), (x - high).astype(BF16)


def dot(left, right, dims):
    return lax.dot_general(left, right, dims, preferred_element_type=F32)


def triple(left, right, dims):
    return (
        dot(left[0], right[0], dims) + dot(left[0], right[1], dims) + dot(left[1], right[0], dims)
    )


REAL, IMAG, MINUS, MOD_REAL, MOD_IMAG = range(5)


def prepare(place_ref, pieces, cs_ref, lefts):
    n = lefts[0].shape[0] // len(pieces)
    cosine, sine = cs_ref[0:1, :], cs_ref[1:2, :]
    for k, piece in enumerate(pieces):
        rows = pl.ds(pl.multiple_of(place_ref[k] * n, n), n)
        real, imag = piece[0, 0:n, :], piece[1, 0:n, :]
        for where, value in (
            (REAL, real),
            (IMAG, imag),
            (MINUS, -imag),
            (MOD_REAL, real * cosine + imag * sine),
            (MOD_IMAG, imag * cosine - real * sine),
        ):
            lefts[2 * where][rows, :], lefts[2 * where + 1][rows, :] = split(value)


def half_product(h, lefts, acc_ref, out_ref):
    elems = lefts[0].shape[0]
    half = elems // 2
    mine = pl.ds(pl.multiple_of(h * half, half), half)
    others = pl.ds(pl.multiple_of((1 - h) * half, half), half)
    everything = pl.ds(0, elems)

    def rows(where, at):
        return tuple(lefts[2 * where + part][at, :] for part in range(2))

    def put(top, cols, value):
        at = (pl.ds(top, half), cols)
        if acc_ref is not None:
            value = value + acc_ref[at]
        out_ref[at] = value

    def real_part(left, at):
        return triple(left[0], rows(REAL, at), NT) + triple(left[1], rows(IMAG, at), NT)

    def imag_part(left, at):
        return triple(left[1], rows(REAL, at), NT) + triple(left[0], rows(MINUS, at), NT)

    mod = (rows(MOD_REAL, mine), rows(MOD_IMAG, mine))
    put(0, everything, real_part(mod, everything))
    put(half, everything, imag_part(mod, everything))
    above = lax.broadcasted_iota(jnp.int32, (half, half), 0) <= lax.broadcasted_iota(
        jnp.int32, (half, half), 1
    )
    plain = (rows(REAL, mine), rows(IMAG, mine))
    put(2 * half, mine, jnp.where(above, real_part(plain, mine), imag_part(plain, mine)))

    @pl.when(h == 0)
    def _():
        put(2 * half, others, real_part(plain, others))

    @pl.when(h != 0)
    def _():
        put(2 * half, others, imag_part(plain, others))


def gram_kernel(has_acc, place_ref, core_ref, *refs):
    pieces, cs_ref, refs = refs[:4], refs[4], refs[5:]
    accs, refs = (refs[:2], refs[2:]) if has_acc else ((None, None), refs)
    prepare(place_ref, pieces, cs_ref, refs[2:])
    half_product(1 - core_ref[0], refs[2:], accs[0], refs[0])
    half_product(core_ref[0], refs[2:], accs[1], refs[1])


SMEM_SPEC = pl.BlockSpec(memory_space=pltpu.SMEM)
VMEM_SPEC = pl.BlockSpec(memory_space=pltpu.VMEM)
MIB = 1 << 20


def gram(elems, place, core, pieces, cs, accs):
    count = pieces[0].shape[2]
    args = [*pieces, cs, *(accs or ())]
    return pl.pallas_call(
        lambda *refs: gram_kernel(accs is not None, *refs),
        out_shape=[jax.ShapeDtypeStruct((3 * elems // 2, elems), F32)] * 2,
        in_specs=[SMEM_SPEC] * 2 + [VMEM_SPEC] * len(args),
        out_specs=[VMEM_SPEC] * 2,
        scratch_shapes=[pltpu.VMEM((elems, count), BF16)] * 10,
        input_output_aliases={7: 0, 8: 1} if accs else {},
        compiler_params=pltpu.CompilerParams(vmem_limit_bytes=24 * MIB),
        cost_estimate=pl.CostEstimate(
            flops=42 * elems * elems * count, bytes_accessed=16 * elems * elems, transcendentals=0
        ),
        name="gram",
    )(place, core, *args)


def add_split_kernel(cut, flags_ref, *refs):
    count = len(refs) // (2 + 2 * cut)
    outs = refs[2 * count :]
    for i in range(count):
        x, y = refs[2 * i], refs[2 * i + 1]
        half = x.shape[0] // (2 * cut)
        for part in range(cut):
            at = i * cut + part
            for side in range(2):
                chosen = flags_ref[at] if side == 0 else 1 - flags_ref[at]
                rows = pl.ds(pl.multiple_of((2 * part + chosen) * half, half), half)
                outs[2 * at + side][...] = x[rows, :] + y[rows, :]


def add_choose_kernel(flag_ref, a, b, c, d, kept_ref, sent_ref):
    @pl.when(flag_ref[0] == 0)
    def _():
        kept_ref[...] = a[...] + b[...]
        sent_ref[...] = c[...] + d[...]

    @pl.when(flag_ref[0] != 0)
    def _():
        kept_ref[...] = c[...] + d[...]
        sent_ref[...] = a[...] + b[...]


def add_choose(flag, *pairs):
    return pl.pallas_call(
        add_choose_kernel,
        out_shape=[jax.ShapeDtypeStruct(pairs[0].shape, F32)] * 2,
        in_specs=[SMEM_SPEC] + [VMEM_SPEC] * 4,
        out_specs=[VMEM_SPEC] * 2,
        compiler_params=pltpu.CompilerParams(vmem_limit_bytes=8 * MIB),
        name="add_choose",
    )(flag[None], *pairs)


def add_split(cut, flags, *pairs):
    shape = (pairs[0].shape[0] // (2 * cut), pairs[0].shape[1])
    if shape[0] % 8:
        sums = [x + y for x, y in zip(pairs[0::2], pairs[1::2])]
        parts = [part for x in sums for part in jnp.split(x, cut)]
        return tuple(
            [
                lax.dynamic_slice_in_dim(part, jnp.abs(side - flags[at]) * shape[0], shape[0], 0)
                for at, part in enumerate(parts)
            ]
            for side in range(2)
        )
    out = pl.pallas_call(
        lambda *refs: add_split_kernel(cut, *refs),
        out_shape=[jax.ShapeDtypeStruct(shape, F32)] * (len(pairs) * cut),
        in_specs=[SMEM_SPEC] + [VMEM_SPEC] * len(pairs),
        out_specs=[VMEM_SPEC] * (len(pairs) * cut),
        compiler_params=pltpu.CompilerParams(vmem_limit_bytes=12 * MIB),
        name="add_split",
    )(flags, *pairs)
    return out[0::2], out[1::2]


def power_kernel(total, core_ref, *refs):
    parts, v_ref, out_ref = refs[:4], refs[4], refs[5]
    cr, ci, pr, pi, packed_ref = refs[6:8], refs[8:10], refs[10:12], refs[12:14], refs[14]
    elems = v_ref.shape[1] // 2
    half = elems // 2
    beams = v_ref.shape[0]
    rows = 2 * beams
    scale = 1.0 / math.sqrt(total * elems)

    for other in range(2):
        h = core_ref[0] if other == 0 else 1 - core_ref[0]
        for part in range(2):
            ref = parts[2 * other + part]
            length = ref.shape[0]
            for begin in range(0, length, half // 2):
                row = part * length + begin
                at = pl.ds(pl.multiple_of(h * half, half) + row % half, half // 2)
                value = ref[pl.ds(begin, half // 2), :]
                if row < 2 * half:
                    pair = cr if row < half else ci
                    pair[0][at, :], pair[1][at, :] = split(value * scale)
                else:
                    packed_ref[at, :] = value * (1.0 / total)

    def store(pair, value):
        pair[0][...], pair[1][...] = split(value)

    packed = packed_ref[...]
    mirrored = packed.T
    row = lax.broadcasted_iota(jnp.int32, (elems, elems), 0)
    col = lax.broadcasted_iota(jnp.int32, (elems, elems), 1)
    store(pr, jnp.where(row <= col, packed, mirrored))
    store(pi, jnp.where(row > col, packed, jnp.where(row < col, -mirrored, 0.0)))

    def normalized(v):
        squares = jnp.sum(v * v, axis=1, keepdims=True)
        squares = squares[:beams] + squares[beams:]
        inverse = 1.0 / jnp.sqrt(squares + EPS)
        return v * jnp.concatenate([inverse, inverse], 0)

    def times(v, pair, dims):
        high, low = split(v)
        both = dot(jnp.concatenate([high, low], 0), pair[0][...], dims)
        return both[:rows] + both[rows:] + dot(high, pair[1][...], dims)

    v = normalized(jnp.concatenate([v_ref[:, 0:elems], v_ref[:, elems:]], 0) - 4.5)
    for _ in range(ITERS):
        by_real = times(v, cr, NN)
        by_imag = times(v, ci, NN)
        w = jnp.concatenate(
            [by_real[:beams] + by_imag[beams:], by_real[beams:] - by_imag[:beams]], 0
        )
        by_real = times(w, cr, NT) + times(v, pr, NT)
        by_imag = times(w, ci, NT) + times(v, pi, NT)
        v = normalized(
            jnp.concatenate(
                [by_real[:beams] - by_imag[beams:], by_real[beams:] + by_imag[:beams]], 0
            )
        )
    out_ref[...] = v


def power(total, core, parts, start):
    rows, elems = 2 * start.shape[0], start.shape[1] // 2
    return pl.pallas_call(
        lambda *refs: power_kernel(total, *refs),
        out_shape=jax.ShapeDtypeStruct((rows, elems), F32),
        in_specs=[SMEM_SPEC] + [VMEM_SPEC] * 5,
        out_specs=VMEM_SPEC,
        scratch_shapes=[pltpu.VMEM((elems, elems), BF16)] * 8 + [pltpu.VMEM((elems, elems), F32)],
        compiler_params=pltpu.CompilerParams(vmem_limit_bytes=24 * MIB),
        cost_estimate=pl.CostEstimate(
            flops=ITERS * 36 * elems * elems * rows, bytes_accessed=16 * elems * elems, transcendentals=0
        ),
        name="power",
    )(core, *parts, start)


def beam_kernel(place_ref, v_ref, *refs):
    pieces, out_ref = refs[:-1], refs[-1]
    rows = v_ref.shape[0]
    beams = rows // 2
    n = v_ref.shape[1] // 4
    count = pieces[0].shape[2]
    lefts = []
    for k in range(4):
        v = v_ref[:, pl.ds(pl.multiple_of(place_ref[k] * n, n), n)]
        high, low = split(v)
        lefts.append((jnp.concatenate([high, low], 0), high))
    for chunk in range(len(pieces) // 4):
        totals = []
        for half in range(2):
            total = 0.0
            for k in range(4):
                high, low = split(pieces[4 * chunk + k][half, 0:n, :])
                both = dot(lefts[k][0], high, NN)
                total = total + (both[:rows] + both[rows:] + dot(lefts[k][1], low, NN))
            totals.append(total)
        by_real, by_imag = totals
        cols = pl.ds(chunk * count, count)
        out_ref[0, :, cols] = by_real[:beams] + by_imag[beams:]
        out_ref[1, :, cols] = by_imag[:beams] - by_real[beams:]


def beams_of(place, v, pieces):
    beams = v.shape[0] // 2
    count = pieces[0].shape[2] * (len(pieces) // 4)
    return pl.pallas_call(
        beam_kernel,
        out_shape=jax.ShapeDtypeStruct((2, beams, count), F32),
        in_specs=[SMEM_SPEC] + [VMEM_SPEC] * (1 + len(pieces)),
        out_specs=VMEM_SPEC,
        compiler_params=pltpu.CompilerParams(vmem_limit_bytes=24 * MIB),
        name="beams",
    )(place, v, *pieces)


def dft_kernel(place_ref, *refs):
    pieces = refs[:4]
    ch, cl, sh, sl, out_ref = refs[4:]
    rows, count = pieces[0].shape[1:]
    width = ch.shape[1]
    phase = lax.broadcasted_iota(jnp.int32, (2 * rows, count), 1) % 4
    by_cos, by_sin = 0.0, 0.0
    for k, piece in enumerate(pieces):
        where = pl.ds(pl.multiple_of(place_ref[k] * count, count), count)
        w = jnp.concatenate([piece[0], piece[1]], 0)
        high, low = split(jnp.concatenate([jnp.where(phase == j, w, 0.0) for j in range(4)], 0))
        by_cos = by_cos + triple((high, low), (ch[where, :], cl[where, :]), NN)
        by_sin = by_sin + triple((high, low), (sh[where, :], sl[where, :]), NN)
    real, imag = [], []
    for j in range(4):
        top, mid, end = 2 * rows * j, 2 * rows * j + rows, 2 * rows * (j + 1)
        real.append(by_cos[top:mid] + by_sin[mid:end])
        imag.append(by_cos[mid:end] - by_sin[top:mid])
    for q in range(4):
        total_real, total_imag = 0.0, 0.0
        for j in range(4):
            turned = (
                (real[j], imag[j]),
                (imag[j], -real[j]),
                (-real[j], -imag[j]),
                (-imag[j], real[j]),
            )[q * j % 4]
            total_real, total_imag = total_real + turned[0], total_imag + turned[1]
        out_ref[0, :, pl.ds(q * width, width)] = total_real
        out_ref[1, :, pl.ds(q * width, width)] = total_imag


def dft(place, pieces, tables):
    rows = pieces[0].shape[1]
    channels = tables[0].shape[0]
    return pl.pallas_call(
        dft_kernel,
        out_shape=jax.ShapeDtypeStruct((2, rows, channels), F32),
        in_specs=[SMEM_SPEC] + [VMEM_SPEC] * 8,
        out_specs=VMEM_SPEC,
        compiler_params=pltpu.CompilerParams(vmem_limit_bytes=16 * MIB),
        name="dft",
    )(place, *pieces, *tables)


def rotation(shift_bin, times, modulus):
    folded = shift_bin[0] * times % modulus
    angle = 2.0 * math.pi / modulus * folded.astype(F32)
    return jnp.stack([jnp.cos(angle), jnp.sin(angle)])


def dft_tables(channels, width):
    step = 32
    f = lax.iota(jnp.int32, width)[None, :]

    def rows(count, factor):
        k = factor * lax.iota(jnp.int32, count)[:, None] * f % channels
        angle = 2.0 * math.pi / channels * k.astype(F32)
        return jnp.cos(angle), jnp.sin(angle)

    coarse, fine = rows(channels // step, step), rows(step, 1)
    a_cos, a_sin = (t[:, None, :] for t in coarse)
    b_cos, b_sin = (t[None, :, :] for t in fine)
    norm = 1.0 / math.sqrt(channels)
    cosine = ((a_cos * b_cos - a_sin * b_sin) * norm).reshape(channels, width)
    sine = ((a_sin * b_cos + a_cos * b_sin) * norm).reshape(channels, width)
    return (*split_kept(cosine), *split_kept(sine))


def share_of_start(start_vectors, width):
    shares, index = lax.axis_size("tm"), lax.axis_index("tm")
    rows = start_vectors.astype(F32).transpose(0, 2, 1)
    count = rows.shape[1] // shares
    rows = lax.dynamic_slice_in_dim(rows, index * count, count, 1)
    return jnp.pad(rows, ((0, 0), (0, -count % 8), (0, width - rows.shape[2])))


def gathered_start(pieces, place, n, beams):
    count = beams // lax.axis_size("tm")
    joint = jnp.zeros((2, count, n * len(pieces)), F32)
    for k, piece in enumerate(pieces):
        share = piece[:, n : n + count, 0:n]
        joint = lax.dynamic_update_slice(joint, share, (0, 0, place[k] * n))
    joint = jnp.concatenate([joint[0], joint[1]], 1)
    for bit in bits("tm"):
        joint = gather_step(joint, "tm", bit)
    return joint


def body(samples, shift_bin, start_vectors, tap_table):
    taps_count, channels = tap_table.shape
    elems_dev, span_len = samples.shape[1:]
    devices = lax.axis_size("elem")
    modulus = span_len * lax.axis_size("tm")
    frames = span_len // channels
    quarter = channels // devices
    mine = lax.axis_index("elem")
    span_start = lax.axis_index("tm") * span_len
    place = jnp.stack([mine ^ k for k in range(devices)])
    core = (lax.axis_index("tm") & 1)[None]

    chunks = []
    accs = None
    late = samples
    for frame in range(frames):
        own = []
        for k in range(devices):
            begin = frame * channels + (mine ^ k) * quarter
            own.append(lax.dynamic_slice_in_dim(late, begin, quarter, 2))
        if frame == 0:
            share = share_of_start(start_vectors, quarter)
            own = [jnp.concatenate([part, share], 1) for part in own]
            late, own = lax.optimization_barrier((late, own))
        pieces = own[:1]
        for k in range(1, devices):
            pieces.append(crossed(own[k], "elem", k))
        times = span_start + frame * channels + mine * quarter + lax.iota(jnp.int32, quarter)
        rotated = rotation(shift_bin, times, modulus)
        if frame == min(1, frames - 1):
            tables, start = dft_tables(channels, quarter), gathered_start(
                chunks[0], place, elems_dev, start_vectors.shape[2]
            )
            rotated, tables, start = lax.optimization_barrier((rotated, tables, start))
        accs = gram(elems_dev * devices, place, core, pieces, rotated, accs)
        chunks.append(pieces)
    sent, kept = accs

    own_parts, other_parts = summed_everywhere(kept, sent)
    v = power(modulus, core, (*own_parts, *other_parts), start)
    beams = v.shape[0] // 2
    weights = (
        lax.dynamic_slice_in_dim(v, mine * elems_dev, elems_dev, 1)
        .reshape(2, beams, elems_dev)
        .transpose(0, 2, 1)
    )
    b = beams_of(place, v, [piece for pieces in chunks for piece in pieces])
    extended = jnp.concatenate([from_behind(b[:, :, -(taps_count - 1) * quarter :], "tm", 1), b], 2)
    taps = lax.dynamic_slice_in_dim(tap_table, mine * quarter, quarter, 1).astype(F32) / 2048.0
    folded = []
    for frame in range(frames):
        w = 0.0
        for tap in range(taps_count):
            at = taps_count - 1 + frame - tap
            w = w + taps[tap] * extended[:, :, at * quarter : (at + 1) * quarter]
        folded.append(w)
    folded = jnp.stack(folded, 1)
    beams_dev = beams // devices
    received = []
    for k in range(devices):
        part = lax.dynamic_slice_in_dim(folded, (mine ^ k) * beams_dev, beams_dev, 2)
        part = part.reshape(2, frames * beams_dev, quarter)
        received.append(part if k == 0 else crossed(part, "elem", k))
    spectra = dft(place, received, tables)
    spectra = spectra.reshape(2, frames, beams_dev, channels).transpose(0, 2, 1, 3)
    return (spectra, weights.reshape(2, elems_dev, beams))


def solution(mesh):
    return jax.shard_map(
        body,
        mesh=mesh,
        in_specs=(P(None, "elem", "tm"), P(), P(None, "elem", None), P()),
        out_specs=(P(None, "elem", "tm", None), P(None, "elem", None)),
        check_vma=False,
    )
```
